32 devices in a mesh: gx: 4 (over z), gy: 8 (over y, x, core).
Axes of the slice: x: 2, y: 2, z: 4, core: 2. Of those that a mesh axis runs over, the one named last changes fastest.
Arguments:
- heat_source: float32 [1536, 1024], P(('gx', 'gy')), may hold values from -18 to 18
- stiffness: float32 [512, 384, 384], P(('gx', 'gy')), may hold values from -1 to 32, as said below
- element_faces: int32 [512, 6], P(('gx', 'gy')), may hold values from 0 to 1535, as said below
Outputs:
- solution: float32 [1536, 1024], P(('gx', 'gy'))
- residual: float32 [1536, 1024], P(('gx', 'gy'))
The draws below stay inside these ranges and needn't reach their ends.
Inputs may be any that keep to these rules, and one draw needn't show every extreme that they name: `element_faces`: the elements form a periodic grid of 8 x 16 x 4 hexahedra; device (i, j) of gx and gy holds the block of 2 x 2 x 4 elements at streamwise block i and spanwise block j, in a local order of its own, and owns the lower x, lower y and lower z faces of its elements, numbered in an order of its own. So every face number appears exactly twice, and a device's elements reference faces of itself, of the next device along gx (cyclic, same gy index; exactly 8 references) and of the next device along gy (cyclic, same gx index; exactly 8 references). `stiffness`: each element matrix is symmetric with a positive diagonal and strictly diagonally dominant.
All inputs are finite; a program needn't handle non-finite values.
Results may differ from the reference program's by a relative error of at most 0.0002.
Values sent between devices are 32-bit elements; how exact they have to be, the bound alone decides.
A program may use at most 128 MiB of HBM per device.

```python
import math
import jax
import jax.numpy as jnp
from jax import lax

BLOCK = 64
EX = 2
EY = 2
EZ = 4
SOURCES = 16
ITERS = 3
E_DEV = 16
FACE_DEV = 48
SPAN_X = 8
SPAN_Y = 16
ELEMENTS = 512
FACES = 1536


def draw_heat_source(key, part):
    device_count = FACES // FACE_DEV
    row_device = (jnp.arange(FACES) // FACE_DEV).astype(jnp.float32)
    device_ramp = (1.0 + 2.0 * row_device / max(device_count - 1, 1))[:, None]
    base_draw = jax.random.truncated_normal(key, -6.0, 6.0, (FACES, SOURCES * BLOCK), jnp.float32)
    return base_draw * device_ramp


def draw_stiffness(key, part):
    block_order = 6 * BLOCK
    identity = jnp.eye(block_order, dtype=jnp.float32)
    diag_high = 2.0
    scale_high = math.log(8.0)

    def draw_element(element_index):
        sub_key = jax.random.fold_in(key, element_index)
        key_off = jax.random.fold_in(sub_key, 1)
        key_diag = jax.random.fold_in(sub_key, 2)
        key_scale = jax.random.fold_in(sub_key, 3)
        weights = jax.random.uniform(key_off, (block_order, block_order), jnp.float32, -1.0, 3.0)
        weights = 0.5 * (weights + weights.T)
        diagonal = jax.random.uniform(key_diag, (block_order, 1), jnp.float32, 1.0, diag_high)
        element_scale = jnp.exp(jax.random.uniform(key_scale, (), jnp.float32, 0.0, scale_high))
        return element_scale * (identity * diagonal + (1.0 - identity) * (-0.3 / block_order) * weights)
    return lax.map(draw_element, jnp.arange(ELEMENTS))


def draw_element_faces(key, part):
    device_count = ELEMENTS // E_DEV
    inner = SPAN_Y // EY
    cell_keys = jax.random.split(jax.random.fold_in(key, 21), device_count)
    face_keys = jax.random.split(jax.random.fold_in(key, 22), device_count)
    cell_orders = jax.vmap(lambda sub_key: jax.random.permutation(sub_key, E_DEV))(cell_keys).astype(jnp.int32)
    face_orders = jax.vmap(lambda sub_key: jax.random.permutation(sub_key, 3 * E_DEV))(face_keys).astype(jnp.int32)
    element_ids = jnp.arange(ELEMENTS, dtype=jnp.int32)
    device_ids = element_ids // E_DEV
    cell = cell_orders[device_ids, element_ids % E_DEV]
    local_x = cell // (EY * EZ)
    local_y = cell // EZ % EY
    local_z = cell % EZ
    place_x = device_ids // inner * EX + local_x
    place_y = device_ids % inner * EY + local_y

    def face_of(spot_x, spot_y, spot_z, kind):
        spot_x = spot_x % SPAN_X
        spot_y = spot_y % SPAN_Y
        spot_z = spot_z % EZ
        owner = spot_x // EX * inner + spot_y // EY
        owner_cell = (spot_x % EX * EY + spot_y % EY) * EZ + spot_z
        return owner * FACE_DEV + face_orders[owner, owner_cell * 3 + kind]
    columns = [face_of(place_x, place_y, local_z, 0), face_of(place_x + 1, place_y, local_z, 0), face_of(place_x, place_y, local_z, 1), face_of(place_x, place_y + 1, local_z, 1), face_of(place_x, place_y, local_z, 2), face_of(place_x, place_y, local_z + 1, 2)]
    return jnp.stack(columns, axis=1).astype(jnp.int32)


def setup_inputs(seed: int = 0) -> dict:
    key_of = jax.random.split(jax.random.key(seed), 4)
    heat_source = draw_heat_source(jax.random.fold_in(key_of[3], 71), 0)
    stiffness = draw_stiffness(jax.random.fold_in(key_of[3], 71), 0)
    element_faces = draw_element_faces(jax.random.fold_in(key_of[3], 71), 0)
    return dict(heat_source=heat_source, stiffness=stiffness, element_faces=element_faces)


def operate(vector, stiffness, element_faces):
    face_count = vector.shape[0]
    flat_faces = element_faces.reshape(-1).astype(jnp.int32)
    blocks = vector[flat_faces].reshape(ELEMENTS, 6, SOURCES, BLOCK)
    matrix = stiffness.reshape(ELEMENTS, 6, BLOCK, 6, BLOCK)
    flux_terms = jnp.einsum("ekbjc,ejsc->eksb", matrix, blocks, precision=lax.Precision.HIGHEST, preferred_element_type=jnp.float32)
    return jax.ops.segment_sum(flux_terms.reshape(ELEMENTS * 6, SOURCES * BLOCK), flat_faces, num_segments=face_count)


def source_sum(first_vec, second_vec):
    return jnp.sum((first_vec * second_vec).reshape(-1, SOURCES, BLOCK), axis=(0, 2))


def spread(per_source):
    return jnp.repeat(per_source, BLOCK)[None, :]


def reference(heat_source, stiffness, element_faces):
    solution = jnp.zeros_like(heat_source)
    residual = heat_source
    direction = heat_source
    norm_now = source_sum(residual, residual)
    for iteration in range(ITERS):
        applied = operate(direction, stiffness, element_faces)
        step_size = norm_now / source_sum(direction, applied)
        solution = solution + spread(step_size) * direction
        residual = residual - spread(step_size) * applied
        norm_next = source_sum(residual, residual)
        direction = residual + spread(norm_next / norm_now) * direction
        norm_now = norm_next
    return solution, residual
```

```python
import jax
import jax.numpy as jnp
from jax import lax
from jax.experimental import pallas as pl
from jax.experimental.pallas import tpu as pltpu
from jax.sharding import PartitionSpec as P

BLOCK = 64
EX = 2
EY = 2
EZ = 4
HALF = BLOCK
LANES = 2 * BLOCK
F32 = jnp.float32
BF16 = jnp.bfloat16
MESH = pl.DeviceIdType.MESH
UNROLL = 2


def index_tables(faces, base, count, face_dev, nx, ny, idx):
    sub = lax.broadcasted_iota(jnp.int32, (count, count), 0)
    lane = lax.broadcasted_iota(jnp.int32, (count, count), 1)
    eye = sub == lane
    slots = 6 * count
    cols = [faces[:, k : k + 1] for k in range(6)]
    rows = [jnp.sum(jnp.where(eye, c, 0), axis=0, keepdims=True) for c in cols]
    idx[...] = jnp.zeros(idx.shape, jnp.int32)
    sizes = [nx, nx, ny, ny]
    starts = [slots, slots + nx, slots + 2 * nx, slots + 2 * nx + ny]
    for axis in range(3):
        low, up = 2 * axis, 2 * axis + 1
        for k, other in ((low, up), (up, low)):
            match = (cols[other] == rows[k]).astype(jnp.int32)
            has = jnp.sum(match, axis=0, keepdims=True)
            place = jnp.sum(match * (other * count + sub), axis=0, keepdims=True)
            local = rows[k] - base
            if axis == 2:
                idx[k : k + 1, 0:count] = place
                idx[6 + k : 7 + k, 0:count] = local
                continue
            match_c = (cols[k] == rows[other]).astype(jnp.int32)
            has_c = jnp.sum(match_c, axis=1, keepdims=True)
            before = jnp.where((has_c == 0) & (cols[k] < rows[k]), 1, 0)
            rank = jnp.sum(before, axis=0, keepdims=True)
            before_c = jnp.where((has == 0) & (rows[k] < cols[k]), 1, 0)
            rank_c = jnp.sum(before_c, axis=1, keepdims=True)
            chosen = (has_c == 0) & (rank_c == lane)
            listed = jnp.sum(jnp.where(chosen, k * count + sub, 0), axis=0, keepdims=True)
            idx[k : k + 1, 0:count] = jnp.where(has > 0, place, starts[k] + rank)
            if k == low:
                traces = jnp.where(chosen, cols[k] - base, 0)
                idx[17 + axis : 18 + axis, 0:count] = jnp.sum(traces, axis=0, keepdims=True)
                idx[6 + k : 7 + k, 0:count] = local
            else:
                first = face_dev + (0 if axis == 0 else nx)
                idx[6 + k : 7 + k, 0:count] = jnp.where(has > 0, local, first + rank)
            idx[12 + k : 13 + k, 0:count] = listed
    wide = lax.broadcasted_iota(jnp.int32, (count, LANES), 1)
    wide_sub = lax.broadcasted_iota(jnp.int32, (count, LANES), 0)
    inverse = jnp.zeros((1, LANES), jnp.int32)
    for k in (0, 2, 4):
        owned = (cols[k] - base) == wide
        inverse = inverse + jnp.sum(
            jnp.where(owned, k * count + wide_sub, 0), axis=0, keepdims=True
        )
    idx[16:17, :] = inverse
    idx[0:6, :] = jnp.clip(idx[0:6, :], 0, slots + 2 * (nx + ny) - 1)
    idx[6:12, :] = jnp.clip(idx[6:12, :], 0, face_dev + nx + ny - 1)
    idx[12:17, :] = jnp.clip(idx[12:17, :], 0, slots - 1)
    idx[17:19, :] = jnp.clip(idx[17:19, :], 0, face_dev - 1)


def make_kernel(outer, inner, count, face_dev, groups, nx, ny):
    slots = 6 * count
    lows = (0, 2, 4)

    def kernel(heat_ref, faces_ref, stiff_ref, sol_ref, res_ref,
               raw, high, low, tile_rows, table, v0, v1, v2, flux, q1,
               idx_v, idx, send0, recv0, sends, recvs, txs, rxx, rxy, txy,
               raw_sem, idx_sem, s0_sem, r0_sem, ss_sem, rr_sem,
               xs_sem, xr_sem, ys_sem, yr_sem):
        gx = lax.axis_index("gx")
        gy = lax.axis_index("gy")
        x_next = (lax.rem(gx + 1, outer), gy)
        x_prev = (lax.rem(gx + outer - 1, outer), gy)
        y_next = (gx, lax.rem(gy + 1, inner))
        y_prev = (gx, lax.rem(gy + inner - 1, inner))

        def raw_copy(e):
            return pltpu.make_async_copy(stiff_ref.at[e], raw.at[e], raw_sem.at[e])

        for e in range(count):
            raw_copy(e).start()
        barrier = pltpu.get_barrier_semaphore()
        for d in range(1, outer):
            pl.semaphore_signal(barrier, inc=1, device_id=(lax.rem(gx + d, outer), gy),
                                device_id_type=MESH)
        for d in range(1, inner):
            pl.semaphore_signal(barrier, inc=1, device_id=(gx, lax.rem(gy + d, inner)),
                                device_id_type=MESH)

        base = (gx * inner + gy) * face_dev
        index_tables(faces_ref[...], base, count, face_dev, nx, ny, idx_v)
        to_smem = pltpu.make_async_copy(idx_v, idx, idx_sem)
        to_smem.start()
        for g in range(face_dev // 8):
            for j in range(groups):
                tile_rows[(g * groups + j) * 8 : (g * groups + j + 1) * 8, :] = heat_ref[
                    g * 8 : g * 8 + 8, j * LANES : (j + 1) * LANES
                ]
        for f in range(face_dev):
            start = (f // 8) * groups * 8 + f % 8
            table[f] = tile_rows[pl.ds(start, groups, stride=8), :]
        to_smem.wait()
        for r in range(nx):
            send0[r] = table[idx[17, r]]
        for r in range(ny):
            send0[nx + r] = table[idx[18, r]]
        pl.semaphore_wait(barrier, outer + inner - 2)

        def remote(src, dst, ssem, rsem, device):
            return pltpu.make_async_remote_copy(
                src_ref=src, dst_ref=dst, send_sem=ssem, recv_sem=rsem,
                device_id=device, device_id_type=MESH,
            )

        first = [
            remote(send0.at[pl.ds(0, nx)], recv0.at[pl.ds(0, nx)], s0_sem.at[0], r0_sem.at[0], x_prev),
            remote(send0.at[pl.ds(nx, ny)], recv0.at[pl.ds(nx, ny)], s0_sem.at[1], r0_sem.at[1], y_prev),
        ]
        for c in first:
            c.start()

        def split(e, carry):
            raw_copy(e).wait()
            a = raw[e]
            h = a.astype(BF16)
            high[e] = h
            low[e] = (a - h.astype(F32)).astype(BF16)
            return carry

        lax.fori_loop(0, count, split, 0)
        for c in first:
            c.wait_recv()
        for r in range(nx + ny):
            table[face_dev + r] = recv0[r]

        def start_trace(e, carry):
            for k in range(6):
                v0[k * count + e] = table[idx[6 + k, e]]
            return carry

        lax.fori_loop(0, count, start_trace, 0, unroll=UNROLL)

        left = lax.broadcasted_iota(jnp.int32, (8, LANES), 1) < HALF

        def swap(a):
            return pltpu.roll(a, HALF, 1)

        def multiply(vec):
            def body(e, acc):
                evens, odds = [], []
                tiles = [vec[k * count + e] for k in range(6)]
                for axis in range(3):
                    a, b = tiles[2 * axis], tiles[2 * axis + 1]
                    evens.append(jnp.where(left, a, swap(b)))
                    odds.append(jnp.where(left, swap(a), b))
                x = jnp.concatenate(
                    [jnp.concatenate(evens, axis=1), jnp.concatenate(odds, axis=1)], axis=0
                )
                xh = x.astype(BF16)
                xl = (x - xh.astype(F32)).astype(BF16)
                both = jnp.concatenate([xh, xl], axis=0)
                p = jnp.dot(both, high[e], preferred_element_type=F32)
                q = jnp.dot(xh, low[e], preferred_element_type=F32)
                y = p[0:16] + (p[16:32] + q)
                for axis in range(3):
                    ev = y[0:8, axis * LANES : (axis + 1) * LANES]
                    od = y[8:16, axis * LANES : (axis + 1) * LANES]
                    fa = jnp.where(left, ev, swap(od))
                    fb = jnp.where(left, swap(ev), od)
                    flux[2 * axis * count + e] = fa
                    flux[(2 * axis + 1) * count + e] = fb
                    acc = acc + (fa * tiles[2 * axis] + fb * tiles[2 * axis + 1])
                return acc

            return lax.fori_loop(0, count, body, jnp.zeros((8, LANES), F32), unroll=UNROLL)

        spots = [0, nx, 2 * nx, 2 * nx + ny]
        plan = [(0, nx, x_prev, 1), (1, nx, x_next, 0), (2, ny, y_prev, 3), (3, ny, y_next, 2)]

        def exchange(phase, kinds):
            copies = []
            for kind, rows, target, lands in plan:
                if kind not in kinds:
                    continue
                for r in range(rows):
                    sends[phase, spots[kind] + r] = flux[idx[12 + kind, r]]
                copies.append(
                    remote(
                        sends.at[phase, pl.ds(spots[kind], rows)],
                        recvs.at[phase, pl.ds(spots[lands], rows)],
                        ss_sem.at[phase, kind], rr_sem.at[phase, lands], target,
                    )
                )
                copies[-1].start()
            return copies

        def landed(phase, copies, kinds):
            for c in copies:
                c.wait_recv()
            for kind, rows, _, _ in plan:
                if kind in kinds:
                    for r in range(rows):
                        flux[slots + spots[kind] + r] = recvs[phase, spots[kind] + r]

        def halves(tile):
            even = jnp.sum(jnp.where(left, tile, 0.0), axis=1, keepdims=True)
            odd = jnp.sum(jnp.where(left, 0.0, tile), axis=1, keepdims=True)
            return even, odd

        lane = lax.broadcasted_iota(jnp.int32, (8, LANES), 1)

        def packed(tiles):
            out = jnp.zeros((8, LANES), F32)
            for m, t in enumerate(tiles):
                even, odd = halves(t)
                out = jnp.where(lane == 2 * m, even, out)
                out = jnp.where(lane == 2 * m + 1, odd, out)
            return out

        def unpacked(total, m):
            return jnp.where(left, total[:, 2 * m : 2 * m + 1], total[:, 2 * m + 1 : 2 * m + 2])

        def sum_x_start(turn, value):
            txs[turn] = value
            copies = []
            for d in range(1, outer):
                copies.append(remote(txs.at[turn], rxx.at[turn, d - 1], xs_sem.at[turn, d - 1],
                                     xr_sem.at[turn, d - 1], (lax.rem(gx + d, outer), gy)))
                copies[-1].start()
            return copies

        def sum_x_end(turn, copies):
            for c in copies:
                c.wait_recv()
            out = txs[turn]
            for d in range(1, outer):
                out = out + rxx[turn, d - 1]
            return out

        def sum_y_start(turn, value):
            txy[turn] = value
            copies = []
            for d in range(1, inner):
                copies.append(remote(txy.at[turn], rxy.at[turn, d - 1], ys_sem.at[turn, d - 1],
                                     yr_sem.at[turn, d - 1], (gx, lax.rem(gy + d, inner))))
                copies[-1].start()
            return copies

        def sum_y_end(turn, copies):
            for c in copies:
                c.wait_recv()
            out = txy[turn]
            for d in range(1, inner):
                out = out + rxy[turn, d - 1]
            return out

        zero = jnp.zeros((8, LANES), F32)

        every = (0, 1, 2, 3)
        delta0 = multiply(v0)
        swap1 = exchange(0, every)
        gamma0 = zero
        for k in lows:
            for e in range(count):
                gamma0 = gamma0 + v0[k * count + e] * v0[k * count + e]
        ax1 = sum_x_start(0, packed([gamma0, delta0]))
        landed(0, swap1, every)

        def assemble(dst, e):
            for k in range(6):
                dst[k * count + e] = flux[k * count + e] + flux[idx[k, e]]

        def asm1(e, carry):
            assemble(v1, e)
            return carry

        lax.fori_loop(0, count, asm1, 0, unroll=UNROLL)
        ay1 = sum_y_start(0, sum_x_end(0, ax1))

        dot_g = multiply(v1)
        swap2 = exchange(1, every)
        total = sum_y_end(0, ay1)
        gamma0 = unpacked(total, 0)
        delta0 = unpacked(total, 1)
        alpha0 = gamma0 / delta0
        landed(1, swap2, every)

        def asm2(e, acc):
            acc = list(acc)
            for k in range(6):
                s = k * count + e
                val = flux[s] + flux[idx[k, e]]
                one = v1[s]
                w = one - alpha0 * val
                q1[s] = w
                v2[s] = val
                if k in lows:
                    r1 = v0[s] - alpha0 * one
                    terms = (r1 * r1, r1 * w, w * w, r1 * one, w * one, one * one, w * val)
                    acc = [a + t for a, t in zip(acc, terms)]
            return tuple(acc)

        dots = lax.fori_loop(0, count, asm2, (zero,) * 7, unroll=UNROLL)
        early = packed([*dots, dot_g])

        dot_e = multiply(q1)
        even, odd = halves(dot_e)
        early = jnp.where(lane == 16, even, early)
        early = jnp.where(lane == 17, odd, early)
        ax2 = sum_x_start(1, early)
        swap3 = exchange(2, (1, 3))
        ay2 = sum_y_start(1, sum_x_end(1, ax2))
        landed(2, swap3, (0, 2))

        def asm3(e, carry):
            for k in lows:
                s = k * count + e
                flux[s] = flux[s] + flux[idx[k, e]]
            return carry

        lax.fori_loop(0, count, asm3, 0, unroll=UNROLL)
        total = sum_y_end(1, ay2)
        g1, d1, ww, rv, wv, vv, f, g, ee = [unpacked(total, m) for m in range(9)]
        b0 = g1 / gamma0
        pap = d1 + 2.0 * b0 * rv + b0 * b0 * delta0
        a1 = g1 / pap
        rs = d1 + b0 * rv
        s2 = ww + b0 * (2.0 * wv + b0 * vv)
        g2 = g1 - 2.0 * a1 * rs + a1 * a1 * s2
        b1 = g2 / g1
        rar = d1 - 2.0 * a1 * (ww + b0 * wv) + a1 * a1 * (ee + b0 * (2.0 * f + b0 * g))
        pap2 = rar + 2.0 * b1 * (rs - a1 * s2) + b1 * b1 * pap
        a2 = g2 / pap2

        def finish(fc, carry):
            s = idx[16, fc]
            x0 = v0[s]
            one = v1[s]
            two = v2[s]
            r1 = x0 - alpha0 * one
            w = one - alpha0 * two
            p1 = r1 + b0 * x0
            s1 = w + b0 * one
            r2 = r1 - a1 * s1
            w2 = w - a1 * (flux[s] + b0 * two)
            p2 = r2 + b1 * p1
            sol_ref[fc] = alpha0 * x0 + a1 * p1 + a2 * p2
            res_ref[fc] = r2 - a2 * (w2 + b1 * s1)
            return carry

        lax.fori_loop(0, face_dev, finish, 0, unroll=2)
        for c in [*first, *swap1, *swap2, *swap3, *ax1, *ay1, *ax2, *ay2]:
            c.wait_send()

    return kernel


def local(heat_source, stiffness, element_faces):
    face_dev, width = heat_source.shape
    count, order = stiffness.shape[0], stiffness.shape[1]
    groups = width // LANES
    outer = lax.axis_size("gx")
    inner = lax.axis_size("gy")
    nx, ny = EY * EZ, EX * EZ
    slots = 6 * count
    ext = 2 * (nx + ny)
    tile = (groups, LANES)
    vmem = lambda *s: pltpu.VMEM(s, F32)
    dma = lambda *s: pltpu.SemaphoreType.DMA(s)
    out = jax.ShapeDtypeStruct((face_dev, *tile), F32)
    sol, res = pl.pallas_call(
        make_kernel(outer, inner, count, face_dev, groups, nx, ny),
        name="cg",
        out_shape=(out, out),
        in_specs=[
            pl.BlockSpec(memory_space=pltpu.VMEM),
            pl.BlockSpec(memory_space=pltpu.VMEM),
            pl.BlockSpec(memory_space=pl.ANY),
        ],
        out_specs=(pl.BlockSpec(memory_space=pltpu.VMEM),) * 2,
        scratch_shapes=[
            vmem(count, order, order),
            pltpu.VMEM((count, order, order), BF16),
            pltpu.VMEM((count, order, order), BF16),
            vmem(face_dev * groups, LANES),
            vmem(face_dev + nx + ny, *tile),
            vmem(slots, *tile),
            vmem(slots, *tile),
            vmem(slots, *tile),
            vmem(slots + ext, *tile),
            vmem(slots, *tile),
            pltpu.VMEM((24, LANES), jnp.int32),
            pltpu.SMEM((24, LANES), jnp.int32),
            vmem(nx + ny, *tile),
            vmem(nx + ny, *tile),
            vmem(3, ext, *tile),
            vmem(3, ext, *tile),
            vmem(2, *tile),
            vmem(2, outer - 1, *tile),
            vmem(2, inner - 1, *tile),
            vmem(2, *tile),
            dma(count), pltpu.SemaphoreType.DMA,
            dma(2), dma(2), dma(3, 4), dma(3, 4),
            dma(2, outer - 1), dma(2, outer - 1), dma(2, inner - 1), dma(2, inner - 1),
        ],
        compiler_params=pltpu.CompilerParams(
            collective_id=0, has_side_effects=True, vmem_limit_bytes=48 * 1024 * 1024
        ),
    )(heat_source, element_faces, stiffness)
    return sol.reshape(face_dev, width), res.reshape(face_dev, width)


def solution(mesh):
    return jax.shard_map(
        local,
        mesh=mesh,
        in_specs=(P(("gx", "gy"), None), P(("gx", "gy"), None, None), P(("gx", "gy"), None)),
        out_specs=(P(("gx", "gy"), None), P(("gx", "gy"), None)),
        check_vma=False,
    )
```

```python
import jax
import jax.numpy as jnp
from jax import lax
from jax.experimental import pallas as pl
from jax.experimental.pallas import tpu as pltpu
from jax.sharding import PartitionSpec as P

BLOCK = 64
EX = 2
EY = 2
EZ = 4
HALF = BLOCK
LANES = 2 * BLOCK
F32 = jnp.float32
BF16 = jnp.bfloat16
MESH = pl.DeviceIdType.MESH
UNROLL = 2


def index_tables(faces, base, count, face_dev, nx, ny, idx):
    sub = lax.broadcasted_iota(jnp.int32, (count, count), 0)
    lane = lax.broadcasted_iota(jnp.int32, (count, count), 1)
    eye = sub == lane
    slots = 6 * count
    cols = [faces[:, k : k + 1] for k in range(6)]
    rows = [jnp.sum(jnp.where(eye, c, 0), axis=0, keepdims=True) for c in cols]
    idx[...] = jnp.zeros(idx.shape, jnp.int32)
    sizes = [nx, nx, ny, ny]
    starts = [slots, slots + nx, slots + 2 * nx, slots + 2 * nx + ny]
    for axis in range(3):
        low, up = 2 * axis, 2 * axis + 1
        for k, other in ((low, up), (up, low)):
            match = (cols[other] == rows[k]).astype(jnp.int32)
            has = jnp.sum(match, axis=0, keepdims=True)
            place = jnp.sum(match * (other * count + sub), axis=0, keepdims=True)
            local = rows[k] - base
            if axis == 2:
                idx[k : k + 1, 0:count] = place
                idx[6 + k : 7 + k, 0:count] = local
                continue
            match_c = (cols[k] == rows[other]).astype(jnp.int32)
            has_c = jnp.sum(match_c, axis=1, keepdims=True)
            before = jnp.where((has_c == 0) & (cols[k] < rows[k]), 1, 0)
            rank = jnp.sum(before, axis=0, keepdims=True)
            before_c = jnp.where((has == 0) & (rows[k] < cols[k]), 1, 0)
            rank_c = jnp.sum(before_c, axis=1, keepdims=True)
            chosen = (has_c == 0) & (rank_c == lane)
            listed = jnp.sum(jnp.where(chosen, k * count + sub, 0), axis=0, keepdims=True)
            idx[k : k + 1, 0:count] = jnp.where(has > 0, place, starts[k] + rank)
            if k == low:
                traces = jnp.where(chosen, cols[k] - base, 0)
                idx[17 + axis : 18 + axis, 0:count] = jnp.sum(traces, axis=0, keepdims=True)
                idx[6 + k : 7 + k, 0:count] = local
            else:
                first = face_dev + (0 if axis == 0 else nx)
                idx[6 + k : 7 + k, 0:count] = jnp.where(has > 0, local, first + rank)
            idx[12 + k : 13 + k, 0:count] = listed
    wide = lax.broadcasted_iota(jnp.int32, (count, LANES), 1)
    wide_sub = lax.broadcasted_iota(jnp.int32, (count, LANES), 0)
    inverse = jnp.zeros((1, LANES), jnp.int32)
    for k in (0, 2, 4):
        owned = (cols[k] - base) == wide
        inverse = inverse + jnp.sum(
            jnp.where(owned, k * count + wide_sub, 0), axis=0, keepdims=True
        )
    idx[16:17, :] = inverse
    idx[0:6, :] = jnp.clip(idx[0:6, :], 0, slots + 2 * (nx + ny) - 1)
    idx[6:12, :] = jnp.clip(idx[6:12, :], 0, face_dev + nx + ny - 1)
    idx[12:17, :] = jnp.clip(idx[12:17, :], 0, slots - 1)
    idx[17:19, :] = jnp.clip(idx[17:19, :], 0, face_dev - 1)


def make_kernel(outer, inner, count, face_dev, groups, nx, ny):
    slots = 6 * count
    lows = (0, 2, 4)
    parts = outer * inner

    def kernel(heat_hbm, faces_hbm, stiff_ref, sol_ref, res_ref,
               heat_ref, faces_ref, raw, high, low, diag, tile_rows, table, v0, v1, v2, flux, q1,
               idx_v, idx, send0, recv0, sends, recvs, sum_tx, sum_rx,
               in_sem, raw_sem, idx_sem, s0_sem, r0_sem, ss_sem, rr_sem,
               sum_ss, sum_rs):
        gx = lax.axis_index("gx")
        gy = lax.axis_index("gy")
        x_next = (lax.rem(gx + 1, outer), gy)
        x_prev = (lax.rem(gx + outer - 1, outer), gy)
        y_next = (gx, lax.rem(gy + 1, inner))
        y_prev = (gx, lax.rem(gy + inner - 1, inner))

        get_heat = pltpu.make_async_copy(heat_hbm, heat_ref, in_sem.at[0])
        get_faces = pltpu.make_async_copy(faces_hbm, faces_ref, in_sem.at[1])
        get_faces.start()
        get_heat.start()

        def other(d):
            return (lax.rem(gx + d // inner, outer), lax.rem(gy + d % inner, inner))

        def raw_copy(e):
            return pltpu.make_async_copy(stiff_ref.at[e], raw.at[e], raw_sem.at[e])

        for e in range(count):
            raw_copy(e).start()
        barrier = pltpu.get_barrier_semaphore()
        for d in range(1, parts):
            pl.semaphore_signal(barrier, inc=1, device_id=other(d), device_id_type=MESH)

        base = (gx * inner + gy) * face_dev
        get_faces.wait()
        index_tables(faces_ref[...], base, count, face_dev, nx, ny, idx_v)
        to_smem = pltpu.make_async_copy(idx_v, idx, idx_sem)
        to_smem.start()
        get_heat.wait()
        for g in range(face_dev // 8):
            for j in range(groups):
                tile_rows[(g * groups + j) * 8 : (g * groups + j + 1) * 8, :] = heat_ref[
                    g * 8 : g * 8 + 8, j * LANES : (j + 1) * LANES
                ]
        for f in range(face_dev):
            start = (f // 8) * groups * 8 + f % 8
            table[f] = tile_rows[pl.ds(start, groups, stride=8), :]
        to_smem.wait()
        for r in range(nx):
            send0[r] = table[idx[17, r]]
        for r in range(ny):
            send0[nx + r] = table[idx[18, r]]
        pl.semaphore_wait(barrier, parts - 1)

        def remote(src, dst, ssem, rsem, device):
            return pltpu.make_async_remote_copy(
                src_ref=src, dst_ref=dst, send_sem=ssem, recv_sem=rsem,
                device_id=device, device_id_type=MESH,
            )

        first = [
            remote(send0.at[pl.ds(0, nx)], recv0.at[pl.ds(0, nx)], s0_sem.at[0], r0_sem.at[0], x_prev),
            remote(send0.at[pl.ds(nx, ny)], recv0.at[pl.ds(nx, ny)], s0_sem.at[1], r0_sem.at[1], y_prev),
        ]
        for c in first:
            c.start()

        eye = lax.broadcasted_iota(jnp.int32, (LANES, LANES), 0) == lax.broadcasted_iota(
            jnp.int32, (LANES, LANES), 1
        )

        def split(e, carry):
            raw_copy(e).wait()
            for r in range(3):
                rows = pl.ds(r * LANES, LANES)
                for c in range(3):
                    columns = pl.ds(c * LANES, LANES)
                    a = raw[e, rows, columns]
                    if r == c:
                        diag[e, :, columns] = jnp.sum(
                            jnp.where(eye, a, 0.0), axis=0, keepdims=True
                        )
                        a = jnp.where(eye, 0.0, a)
                    h = a.astype(BF16)
                    high[e, rows, columns] = h
                    low[e, rows, columns] = (a - h.astype(F32)).astype(BF16)
            return carry

        lax.fori_loop(0, count, split, 0)
        for c in first:
            c.wait_recv()
        for r in range(nx + ny):
            table[face_dev + r] = recv0[r]

        def start_trace(e, carry):
            for k in range(6):
                v0[k * count + e] = table[idx[6 + k, e]]
            return carry

        lax.fori_loop(0, count, start_trace, 0, unroll=UNROLL)

        left = lax.broadcasted_iota(jnp.int32, (8, LANES), 1) < HALF

        def swap(a):
            return pltpu.roll(a, HALF, 1)

        def multiply(vec):
            def body(e, acc):
                evens, odds = [], []
                tiles = [vec[k * count + e] for k in range(6)]
                for axis in range(3):
                    a, b = tiles[2 * axis], tiles[2 * axis + 1]
                    evens.append(jnp.where(left, a, swap(b)))
                    odds.append(jnp.where(left, swap(a), b))
                x = jnp.concatenate(
                    [jnp.concatenate(evens, axis=1), jnp.concatenate(odds, axis=1)], axis=0
                )
                xh = x.astype(BF16)
                xl = (x - xh.astype(F32)).astype(BF16)
                both = jnp.concatenate([xh, xl], axis=0)
                p = jnp.dot(both, high[e], preferred_element_type=F32)
                q = jnp.dot(xh, low[e], preferred_element_type=F32)
                y = x * diag[e] + (p[0:16] + (p[16:32] + q))
                for axis in range(3):
                    ev = y[0:8, axis * LANES : (axis + 1) * LANES]
                    od = y[8:16, axis * LANES : (axis + 1) * LANES]
                    fa = jnp.where(left, ev, swap(od))
                    fb = jnp.where(left, swap(ev), od)
                    flux[2 * axis * count + e] = fa
                    flux[(2 * axis + 1) * count + e] = fb
                    acc = acc + (fa * tiles[2 * axis] + fb * tiles[2 * axis + 1])
                return acc

            return lax.fori_loop(0, count, body, jnp.zeros((8, LANES), F32), unroll=UNROLL)

        spots = [0, nx, 2 * nx, 2 * nx + ny]
        plan = [(0, nx, x_prev, 1), (1, nx, x_next, 0), (2, ny, y_prev, 3), (3, ny, y_next, 2)]

        def exchange(phase, kinds):
            copies = []
            for kind, rows, target, lands in plan:
                if kind not in kinds:
                    continue
                for r in range(rows):
                    sends[phase, spots[kind] + r] = flux[idx[12 + kind, r]]
                copies.append(
                    remote(
                        sends.at[phase, pl.ds(spots[kind], rows)],
                        recvs.at[phase, pl.ds(spots[lands], rows)],
                        ss_sem.at[phase, kind], rr_sem.at[phase, lands], target,
                    )
                )
                copies[-1].start()
            return copies

        def landed(phase, copies, kinds):
            for c in copies:
                c.wait_recv()
            for kind, rows, _, _ in plan:
                if kind in kinds:
                    for r in range(rows):
                        flux[slots + spots[kind] + r] = recvs[phase, spots[kind] + r]

        def halves(tile):
            even = jnp.sum(jnp.where(left, tile, 0.0), axis=1, keepdims=True)
            odd = jnp.sum(jnp.where(left, 0.0, tile), axis=1, keepdims=True)
            return even, odd

        lane = lax.broadcasted_iota(jnp.int32, (8, LANES), 1)

        sub = lax.broadcasted_iota(jnp.int32, (8, LANES), 0)
        spot = lane % 16
        mine = lane // 16 == sub

        def packed(tiles, out=None, first=0):
            out = jnp.zeros((8, LANES), F32) if out is None else out
            for m, t in enumerate(tiles, first):
                even, odd = halves(t)
                out = jnp.where(spot == 2 * m, even, out)
                out = jnp.where(spot == 2 * m + 1, odd, out)
            return out

        def unpacked(row, m):
            own = jnp.where(mine, jnp.broadcast_to(row, (8, LANES)), 0.0)
            even = jnp.sum(jnp.where(spot == 2 * m, own, 0.0), axis=1, keepdims=True)
            odd = jnp.sum(jnp.where(spot == 2 * m + 1, own, 0.0), axis=1, keepdims=True)
            return jnp.where(left, even, odd)

        def sum_start(turn, value):
            sum_tx[turn] = jnp.sum(jnp.where(mine, value, 0.0), axis=0, keepdims=True)
            copies = []
            for d in range(1, parts):
                copies.append(remote(sum_tx.at[turn], sum_rx.at[turn, d - 1], sum_ss.at[turn, d - 1],
                                     sum_rs.at[turn, d - 1], other(d)))
                copies[-1].start()
            return copies

        def sum_end(turn, copies):
            for c in copies:
                c.wait_recv()
            return sum_tx[turn] + jnp.sum(sum_rx[turn], axis=0)

        zero = jnp.zeros((8, LANES), F32)

        every = (0, 1, 2, 3)
        delta0 = multiply(v0)
        swap1 = exchange(0, every)
        gamma0 = zero
        for k in lows:
            for e in range(count):
                gamma0 = gamma0 + v0[k * count + e] * v0[k * count + e]
        sum1 = sum_start(0, packed([gamma0, delta0]))
        landed(0, swap1, every)

        def assemble(dst, e):
            for k in range(6):
                dst[k * count + e] = flux[k * count + e] + flux[idx[k, e]]

        def asm1(e, carry):
            assemble(v1, e)
            return carry

        lax.fori_loop(0, count, asm1, 0, unroll=UNROLL)

        dot_g = multiply(v1)
        swap2 = exchange(1, every)
        total = sum_end(0, sum1)
        gamma0 = unpacked(total, 0)
        delta0 = unpacked(total, 1)
        alpha0 = gamma0 / delta0
        landed(1, swap2, every)

        def asm2(e, acc):
            acc = list(acc)
            for k in range(6):
                s = k * count + e
                val = flux[s] + flux[idx[k, e]]
                one = v1[s]
                w = one - alpha0 * val
                q1[s] = w
                v2[s] = val
                if k in lows:
                    r1 = v0[s] - alpha0 * one
                    terms = (r1 * r1, r1 * w, w * w, w * one, one * one, w * val)
                    acc = [a + t for a, t in zip(acc, terms)]
            return tuple(acc)

        dots = lax.fori_loop(0, count, asm2, (zero,) * 6, unroll=UNROLL)
        early = packed([*dots, dot_g])

        dot_e = multiply(q1)
        sum2 = sum_start(1, packed([dot_e], early, 7))
        swap3 = exchange(2, (1, 3))
        landed(2, swap3, (0, 2))

        def asm3(e, carry):
            for k in lows:
                s = k * count + e
                flux[s] = flux[s] + flux[idx[k, e]]
            return carry

        lax.fori_loop(0, count, asm3, 0, unroll=UNROLL)
        total = sum_end(1, sum2)
        g1, d1, ww, wv, vv, f, g, ee = [unpacked(total, m) for m in range(8)]
        rv = -g1 / alpha0
        b0 = g1 / gamma0
        pap = d1 + 2.0 * b0 * rv + b0 * b0 * delta0
        a1 = g1 / pap
        rs = d1 + b0 * rv
        s2 = ww + b0 * (2.0 * wv + b0 * vv)
        g2 = g1 - 2.0 * a1 * rs + a1 * a1 * s2
        b1 = g2 / g1
        rar = d1 - 2.0 * a1 * (ww + b0 * wv) + a1 * a1 * (ee + b0 * (2.0 * f + b0 * g))
        pap2 = rar + 2.0 * b1 * (rs - a1 * s2) + b1 * b1 * pap
        a2 = g2 / pap2

        def finish(fc, carry):
            s = idx[16, fc]
            x0 = v0[s]
            one = v1[s]
            two = v2[s]
            r1 = x0 - alpha0 * one
            w = one - alpha0 * two
            p1 = r1 + b0 * x0
            s1 = w + b0 * one
            r2 = r1 - a1 * s1
            w2 = w - a1 * (flux[s] + b0 * two)
            p2 = r2 + b1 * p1
            sol_ref[fc] = alpha0 * x0 + a1 * p1 + a2 * p2
            res_ref[fc] = r2 - a2 * (w2 + b1 * s1)
            return carry

        lax.fori_loop(0, face_dev, finish, 0, unroll=2)
        for c in [*first, *swap1, *swap2, *swap3, *sum1, *sum2]:
            c.wait_send()

    return kernel


def local(heat_source, stiffness, element_faces):
    face_dev, width = heat_source.shape
    count, order = stiffness.shape[0], stiffness.shape[1]
    groups = width // LANES
    outer = lax.axis_size("gx")
    inner = lax.axis_size("gy")
    nx, ny = EY * EZ, EX * EZ
    slots = 6 * count
    ext = 2 * (nx + ny)
    tile = (groups, LANES)
    vmem = lambda *s: pltpu.VMEM(s, F32)
    dma = lambda *s: pltpu.SemaphoreType.DMA(s)
    out = jax.ShapeDtypeStruct((face_dev, *tile), F32)
    sol, res = pl.pallas_call(
        make_kernel(outer, inner, count, face_dev, groups, nx, ny),
        name="cg",
        out_shape=(out, out),
        in_specs=[
            pl.BlockSpec(memory_space=pltpu.HBM),
            pl.BlockSpec(memory_space=pltpu.HBM),
            pl.BlockSpec(memory_space=pltpu.HBM),
        ],
        out_specs=(pl.BlockSpec(memory_space=pltpu.VMEM),) * 2,
        scratch_shapes=[
            vmem(face_dev, width),
            pltpu.VMEM(element_faces.shape, jnp.int32),
            vmem(count, order, order),
            pltpu.VMEM((count, order, order), BF16),
            pltpu.VMEM((count, order, order), BF16),
            vmem(count, 1, order),
            vmem(face_dev * groups, LANES),
            vmem(face_dev + nx + ny, *tile),
            vmem(slots, *tile),
            vmem(slots, *tile),
            vmem(slots, *tile),
            vmem(slots + ext, *tile),
            vmem(slots, *tile),
            pltpu.VMEM((24, LANES), jnp.int32),
            pltpu.SMEM((24, LANES), jnp.int32),
            vmem(nx + ny, *tile),
            vmem(nx + ny, *tile),
            vmem(3, ext, *tile),
            vmem(3, ext, *tile),
            vmem(2, 1, LANES),
            vmem(2, outer * inner - 1, 1, LANES),
            dma(2),
            dma(count), pltpu.SemaphoreType.DMA,
            dma(2), dma(2), dma(3, 4), dma(3, 4),
            dma(2, outer * inner - 1), dma(2, outer * inner - 1),
        ],
        compiler_params=pltpu.CompilerParams(
            collective_id=0, has_side_effects=True, vmem_limit_bytes=67043328
        ),
    )(heat_source, element_faces, stiffness)
    return sol.reshape(face_dev, width), res.reshape(face_dev, width)


def solution(mesh):
    return jax.shard_map(
        local,
        mesh=mesh,
        in_specs=(P(("gx", "gy"), None), P(("gx", "gy"), None, None), P(("gx", "gy"), None)),
        out_specs=(P(("gx", "gy"), None), P(("gx", "gy"), None)),
        check_vma=False,
    )
```

```python
import jax
import jax.numpy as jnp
from jax import lax
from jax.experimental import pallas as pl
from jax.experimental.pallas import tpu as pltpu
from jax.sharding import PartitionSpec as P

BLOCK = 64
EX = 2
EY = 2
EZ = 4
HALF = BLOCK
LANES = 2 * BLOCK
F32 = jnp.float32
BF16 = jnp.bfloat16
MESH = pl.DeviceIdType.MESH
UNROLL = 2


def index_tables(faces, base, count, face_dev, nx, ny, idx):
    sub = lax.broadcasted_iota(jnp.int32, (count, count), 0)
    lane = lax.broadcasted_iota(jnp.int32, (count, count), 1)
    eye = sub == lane
    slots = 6 * count
    rows = [faces[k : k + 1, :] for k in range(6)]
    cols = [jnp.sum(jnp.where(eye, r, 0), axis=1, keepdims=True) for r in rows]
    idx[...] = jnp.zeros(idx.shape, jnp.int32)
    sizes = [nx, nx, ny, ny]
    starts = [slots, slots + nx, slots + 2 * nx, slots + 2 * nx + ny]
    for axis in range(3):
        low, up = 2 * axis, 2 * axis + 1
        for k, other in ((low, up), (up, low)):
            match = (cols[other] == rows[k]).astype(jnp.int32)
            has = jnp.sum(match, axis=0, keepdims=True)
            place = jnp.sum(match * (other * count + sub), axis=0, keepdims=True)
            local = rows[k] - base
            if axis == 2:
                idx[k : k + 1, 0:count] = place
                idx[6 + k : 7 + k, 0:count] = local
                continue
            match_c = (cols[k] == rows[other]).astype(jnp.int32)
            has_c = jnp.sum(match_c, axis=1, keepdims=True)
            before = jnp.where((has_c == 0) & (cols[k] < rows[k]), 1, 0)
            rank = jnp.sum(before, axis=0, keepdims=True)
            before_c = jnp.where((has == 0) & (rows[k] < cols[k]), 1, 0)
            rank_c = jnp.sum(before_c, axis=1, keepdims=True)
            chosen = (has_c == 0) & (rank_c == lane)
            listed = jnp.sum(jnp.where(chosen, k * count + sub, 0), axis=0, keepdims=True)
            idx[k : k + 1, 0:count] = jnp.where(has > 0, place, starts[k] + rank)
            if k == low:
                traces = jnp.where(chosen, cols[k] - base, 0)
                idx[17 + axis : 18 + axis, 0:count] = jnp.sum(traces, axis=0, keepdims=True)
                idx[6 + k : 7 + k, 0:count] = local
            else:
                first = face_dev + (0 if axis == 0 else nx)
                idx[6 + k : 7 + k, 0:count] = jnp.where(has > 0, local, first + rank)
            idx[12 + k : 13 + k, 0:count] = listed
    wide = lax.broadcasted_iota(jnp.int32, (count, LANES), 1)
    wide_sub = lax.broadcasted_iota(jnp.int32, (count, LANES), 0)
    inverse = jnp.zeros((1, LANES), jnp.int32)
    for k in (0, 2, 4):
        owned = (cols[k] - base) == wide
        inverse = inverse + jnp.sum(
            jnp.where(owned, k * count + wide_sub, 0), axis=0, keepdims=True
        )
    idx[16:17, :] = inverse
    idx[0:6, :] = jnp.clip(idx[0:6, :], 0, slots + 2 * (nx + ny) - 1)
    idx[6:12, :] = jnp.clip(idx[6:12, :], 0, face_dev + nx + ny - 1)
    idx[12:17, :] = jnp.clip(idx[12:17, :], 0, slots - 1)
    idx[17:19, :] = jnp.clip(idx[17:19, :], 0, face_dev - 1)


def make_kernel(outer, inner, count, face_dev, groups, nx, ny):
    slots = 6 * count
    lows = (0, 2, 4)
    parts = outer * inner

    def kernel(heat_hbm, faces_hbm, stiff_ref, sol_ref, res_ref,
               heat_ref, faces_ref, raw, high, low, diag, tile_rows, table, v0, v1, v2, flux, q1,
               idx_v, idx, send0, recv0, sends, recvs, sum_tx, sum_rx,
               in_sem, raw_sem, idx_sem, s0_sem, r0_sem, ss_sem, rr_sem,
               sum_ss, sum_rs):
        gx = lax.axis_index("gx")
        gy = lax.axis_index("gy")
        x_next = (lax.rem(gx + 1, outer), gy)
        x_prev = (lax.rem(gx + outer - 1, outer), gy)
        y_next = (gx, lax.rem(gy + 1, inner))
        y_prev = (gx, lax.rem(gy + inner - 1, inner))

        get_heat = pltpu.make_async_copy(heat_hbm, heat_ref, in_sem.at[0])
        get_faces = pltpu.make_async_copy(faces_hbm, faces_ref, in_sem.at[1])
        get_faces.start()
        get_heat.start()

        def other(d):
            return (lax.rem(gx + d // inner, outer), lax.rem(gy + d % inner, inner))

        def raw_copy(e):
            return pltpu.make_async_copy(stiff_ref.at[e], raw.at[e], raw_sem.at[e])

        for e in range(count):
            raw_copy(e).start()
        barrier = pltpu.get_barrier_semaphore()
        for d in range(1, parts):
            pl.semaphore_signal(barrier, inc=1, device_id=other(d), device_id_type=MESH)

        base = (gx * inner + gy) * face_dev
        get_faces.wait()
        index_tables(faces_ref[...], base, count, face_dev, nx, ny, idx_v)
        to_smem = pltpu.make_async_copy(idx_v, idx, idx_sem)
        to_smem.start()
        get_heat.wait()
        for g in range(face_dev // 8):
            for j in range(groups):
                tile_rows[(g * groups + j) * 8 : (g * groups + j + 1) * 8, :] = heat_ref[
                    g * 8 : g * 8 + 8, j * LANES : (j + 1) * LANES
                ]
        for f in range(face_dev):
            start = (f // 8) * groups * 8 + f % 8
            table[f] = tile_rows[pl.ds(start, groups, stride=8), :]
        to_smem.wait()
        for r in range(nx):
            send0[r] = table[idx[17, r]]
        for r in range(ny):
            send0[nx + r] = table[idx[18, r]]
        pl.semaphore_wait(barrier, parts - 1)

        def remote(src, dst, ssem, rsem, device):
            return pltpu.make_async_remote_copy(
                src_ref=src, dst_ref=dst, send_sem=ssem, recv_sem=rsem,
                device_id=device, device_id_type=MESH,
            )

        first = [
            remote(send0.at[pl.ds(0, nx)], recv0.at[pl.ds(0, nx)], s0_sem.at[0], r0_sem.at[0], x_prev),
            remote(send0.at[pl.ds(nx, ny)], recv0.at[pl.ds(nx, ny)], s0_sem.at[1], r0_sem.at[1], y_prev),
        ]
        for c in first:
            c.start()

        eye = lax.broadcasted_iota(jnp.int32, (LANES, LANES), 0) == lax.broadcasted_iota(
            jnp.int32, (LANES, LANES), 1
        )

        def split(e, carry):
            raw_copy(e).wait()
            for r in range(3):
                rows = pl.ds(r * LANES, LANES)
                for c in range(3):
                    columns = pl.ds(c * LANES, LANES)
                    a = raw[e, rows, columns]
                    if r == c:
                        diag[e, :, columns] = jnp.sum(
                            jnp.where(eye, a, 0.0), axis=0, keepdims=True
                        )
                        a = jnp.where(eye, 0.0, a)
                    h = a.astype(BF16)
                    high[e, rows, columns] = h
                    low[e, rows, columns] = (a - h.astype(F32)).astype(BF16)
            return carry

        lax.fori_loop(0, count, split, 0)
        for c in first:
            c.wait_recv()
        for r in range(nx + ny):
            table[face_dev + r] = recv0[r]

        def start_trace(e, carry):
            for k in range(6):
                v0[k * count + e] = table[idx[6 + k, e]]
            return carry

        lax.fori_loop(0, count, start_trace, 0, unroll=UNROLL)

        left = lax.broadcasted_iota(jnp.int32, (8, LANES), 1) < HALF

        def swap(a):
            return pltpu.roll(a, HALF, 1)

        def multiply(vec):
            def body(e, acc):
                evens, odds = [], []
                tiles = [vec[k * count + e] for k in range(6)]
                for axis in range(3):
                    a, b = tiles[2 * axis], tiles[2 * axis + 1]
                    evens.append(jnp.where(left, a, swap(b)))
                    odds.append(jnp.where(left, swap(a), b))
                x = jnp.concatenate(
                    [jnp.concatenate(evens, axis=1), jnp.concatenate(odds, axis=1)], axis=0
                )
                xh = x.astype(BF16)
                xl = (x - xh.astype(F32)).astype(BF16)
                both = jnp.concatenate([xh, xl], axis=0)
                p = jnp.dot(both, high[e], preferred_element_type=F32)
                q = jnp.dot(xh, low[e], preferred_element_type=F32)
                y = x * diag[e] + (p[0:16] + (p[16:32] + q))
                for axis in range(3):
                    ev = y[0:8, axis * LANES : (axis + 1) * LANES]
                    od = y[8:16, axis * LANES : (axis + 1) * LANES]
                    fa = jnp.where(left, ev, swap(od))
                    fb = jnp.where(left, swap(ev), od)
                    flux[2 * axis * count + e] = fa
                    flux[(2 * axis + 1) * count + e] = fb
                    acc = acc + (fa * tiles[2 * axis] + fb * tiles[2 * axis + 1])
                return acc

            return lax.fori_loop(0, count, body, jnp.zeros((8, LANES), F32), unroll=True)

        spots = [0, nx, 2 * nx, 2 * nx + ny]
        plan = [(0, nx, x_prev, 1), (1, nx, x_next, 0), (2, ny, y_prev, 3), (3, ny, y_next, 2)]

        def exchange(phase, kinds):
            copies = []
            for kind, rows, target, lands in plan:
                if kind not in kinds:
                    continue
                for r in range(rows):
                    sends[phase, spots[kind] + r] = flux[idx[12 + kind, r]]
                copies.append(
                    remote(
                        sends.at[phase, pl.ds(spots[kind], rows)],
                        recvs.at[phase, pl.ds(spots[lands], rows)],
                        ss_sem.at[phase, kind], rr_sem.at[phase, lands], target,
                    )
                )
                copies[-1].start()
            return copies

        def landed(phase, copies, kinds):
            for c in copies:
                c.wait_recv()
            for kind, rows, _, _ in plan:
                if kind in kinds:
                    for r in range(rows):
                        flux[slots + spots[kind] + r] = recvs[phase, spots[kind] + r]

        def halves(tile):
            even = jnp.sum(jnp.where(left, tile, 0.0), axis=1, keepdims=True)
            odd = jnp.sum(jnp.where(left, 0.0, tile), axis=1, keepdims=True)
            return even, odd

        lane = lax.broadcasted_iota(jnp.int32, (8, LANES), 1)

        sub = lax.broadcasted_iota(jnp.int32, (8, LANES), 0)
        spot = lane % 16
        mine = lane // 16 == sub

        def packed(tiles, out=None, first=0):
            out = jnp.zeros((8, LANES), F32) if out is None else out
            for m, t in enumerate(tiles, first):
                even, odd = halves(t)
                out = jnp.where(spot == 2 * m, even, out)
                out = jnp.where(spot == 2 * m + 1, odd, out)
            return out

        def unpacked(row, m):
            own = jnp.where(mine, jnp.broadcast_to(row, (8, LANES)), 0.0)
            even = jnp.sum(jnp.where(spot == 2 * m, own, 0.0), axis=1, keepdims=True)
            odd = jnp.sum(jnp.where(spot == 2 * m + 1, own, 0.0), axis=1, keepdims=True)
            return jnp.where(left, even, odd)

        def sum_start(turn, value):
            sum_tx[turn] = jnp.sum(jnp.where(mine, value, 0.0), axis=0, keepdims=True)
            copies = []
            for d in range(1, parts):
                copies.append(remote(sum_tx.at[turn], sum_rx.at[turn, d - 1], sum_ss.at[turn, d - 1],
                                     sum_rs.at[turn, d - 1], other(d)))
                copies[-1].start()
            return copies

        def sum_end(turn, copies):
            for c in copies:
                c.wait_recv()
            return sum_tx[turn] + jnp.sum(sum_rx[turn], axis=0)

        zero = jnp.zeros((8, LANES), F32)

        every = (0, 1, 2, 3)
        delta0 = multiply(v0)
        swap1 = exchange(0, every)
        gamma0 = zero
        for k in lows:
            for e in range(count):
                gamma0 = gamma0 + v0[k * count + e] * v0[k * count + e]
        sum1 = sum_start(0, packed([gamma0, delta0]))
        landed(0, swap1, every)

        def assemble(dst, e):
            for k in range(6):
                dst[k * count + e] = flux[k * count + e] + flux[idx[k, e]]

        def asm1(e, carry):
            assemble(v1, e)
            return carry

        lax.fori_loop(0, count, asm1, 0, unroll=UNROLL)

        dot_g = multiply(v1)
        swap2 = exchange(1, every)
        total = sum_end(0, sum1)
        gamma0 = unpacked(total, 0)
        delta0 = unpacked(total, 1)
        alpha0 = gamma0 / delta0
        landed(1, swap2, every)

        def asm2(e, acc):
            acc = list(acc)
            for k in range(6):
                s = k * count + e
                val = flux[s] + flux[idx[k, e]]
                one = v1[s]
                w = one - alpha0 * val
                q1[s] = w
                v2[s] = val
                if k in lows:
                    r1 = v0[s] - alpha0 * one
                    terms = (r1 * r1, r1 * w, w * w, w * one, one * one, w * val)
                    acc = [a + t for a, t in zip(acc, terms)]
            return tuple(acc)

        dots = lax.fori_loop(0, count, asm2, (zero,) * 6, unroll=UNROLL)
        early = packed([*dots, dot_g])

        dot_e = multiply(q1)
        sum2 = sum_start(1, packed([dot_e], early, 7))
        swap3 = exchange(2, (1, 3))
        landed(2, swap3, (0, 2))

        def asm3(e, carry):
            for k in lows:
                s = k * count + e
                flux[s] = flux[s] + flux[idx[k, e]]
            return carry

        lax.fori_loop(0, count, asm3, 0, unroll=UNROLL)
        total = sum_end(1, sum2)
        g1, d1, ww, wv, vv, f, g, ee = [unpacked(total, m) for m in range(8)]
        rv = -g1 / alpha0
        b0 = g1 / gamma0
        pap = d1 + 2.0 * b0 * rv + b0 * b0 * delta0
        a1 = g1 / pap
        rs = d1 + b0 * rv
        s2 = ww + b0 * (2.0 * wv + b0 * vv)
        g2 = g1 - 2.0 * a1 * rs + a1 * a1 * s2
        b1 = g2 / g1
        rar = d1 - 2.0 * a1 * (ww + b0 * wv) + a1 * a1 * (ee + b0 * (2.0 * f + b0 * g))
        pap2 = rar + 2.0 * b1 * (rs - a1 * s2) + b1 * b1 * pap
        a2 = g2 / pap2

        def finish(fc, carry):
            s = idx[16, fc]
            x0 = v0[s]
            one = v1[s]
            two = v2[s]
            r1 = x0 - alpha0 * one
            w = one - alpha0 * two
            p1 = r1 + b0 * x0
            s1 = w + b0 * one
            r2 = r1 - a1 * s1
            w2 = w - a1 * (flux[s] + b0 * two)
            p2 = r2 + b1 * p1
            sol_ref[fc] = alpha0 * x0 + a1 * p1 + a2 * p2
            res_ref[fc] = r2 - a2 * (w2 + b1 * s1)
            return carry

        lax.fori_loop(0, face_dev, finish, 0, unroll=2)
        for c in [*first, *swap1, *swap2, *swap3, *sum1, *sum2]:
            c.wait_send()

    return kernel


def local(heat_source, stiffness, element_faces):
    face_dev, width = heat_source.shape
    count, order = stiffness.shape[0], stiffness.shape[1]
    groups = width // LANES
    outer = lax.axis_size("gx")
    inner = lax.axis_size("gy")
    nx, ny = EY * EZ, EX * EZ
    slots = 6 * count
    ext = 2 * (nx + ny)
    tile = (groups, LANES)
    vmem = lambda *s: pltpu.VMEM(s, F32)
    dma = lambda *s: pltpu.SemaphoreType.DMA(s)
    out = jax.ShapeDtypeStruct((face_dev, *tile), F32)
    sol, res = pl.pallas_call(
        make_kernel(outer, inner, count, face_dev, groups, nx, ny),
        name="cg",
        out_shape=(out, out),
        in_specs=[
            pl.BlockSpec(memory_space=pltpu.HBM),
            pl.BlockSpec(memory_space=pltpu.HBM),
            pl.BlockSpec(memory_space=pltpu.HBM),
        ],
        out_specs=(pl.BlockSpec(memory_space=pltpu.VMEM),) * 2,
        scratch_shapes=[
            vmem(face_dev, width),
            pltpu.VMEM((6, count), jnp.int32),
            vmem(count, order, order),
            pltpu.VMEM((count, order, order), BF16),
            pltpu.VMEM((count, order, order), BF16),
            vmem(count, 1, order),
            vmem(face_dev * groups, LANES),
            vmem(face_dev + nx + ny, *tile),
            vmem(slots, *tile),
            vmem(slots, *tile),
            vmem(slots, *tile),
            vmem(slots + ext, *tile),
            vmem(slots, *tile),
            pltpu.VMEM((24, LANES), jnp.int32),
            pltpu.SMEM((24, LANES), jnp.int32),
            vmem(nx + ny, *tile),
            vmem(nx + ny, *tile),
            vmem(3, ext, *tile),
            vmem(3, ext, *tile),
            vmem(2, 1, LANES),
            vmem(2, outer * inner - 1, 1, LANES),
            dma(2),
            dma(count), pltpu.SemaphoreType.DMA,
            dma(2), dma(2), dma(3, 4), dma(3, 4),
            dma(2, outer * inner - 1), dma(2, outer * inner - 1),
        ],
        compiler_params=pltpu.CompilerParams(
            collective_id=0, has_side_effects=True, vmem_limit_bytes=67043328
        ),
    )(heat_source, element_faces.T, stiffness)
    return sol.reshape(face_dev, width), res.reshape(face_dev, width)


def solution(mesh):
    return jax.shard_map(
        local,
        mesh=mesh,
        in_specs=(P(("gx", "gy"), None), P(("gx", "gy"), None, None), P(("gx", "gy"), None)),
        out_specs=(P(("gx", "gy"), None), P(("gx", "gy"), None)),
        check_vma=False,
    )
```

```python
import jax
import jax.numpy as jnp
from jax import lax
from jax.experimental import pallas as pl
from jax.experimental.pallas import tpu as pltpu
from jax.sharding import PartitionSpec as P

BLOCK = 64
EX = 2
EY = 2
EZ = 4
HALF = BLOCK
LANES = 2 * BLOCK
F32 = jnp.float32
BF16 = jnp.bfloat16
MESH = pl.DeviceIdType.MESH
UNROLL = 2


def index_tables(faces, base, count, face_dev, nx, ny, idx):
    sub = lax.broadcasted_iota(jnp.int32, (count, count), 0)
    lane = lax.broadcasted_iota(jnp.int32, (count, count), 1)
    eye = sub == lane
    slots = 6 * count
    rows = [faces[k : k + 1, :] for k in range(6)]
    cols = [jnp.sum(jnp.where(eye, r, 0), axis=1, keepdims=True) for r in rows]
    idx[...] = jnp.zeros(idx.shape, jnp.int32)
    sizes = [nx, nx, ny, ny]
    starts = [slots, slots + nx, slots + 2 * nx, slots + 2 * nx + ny]
    for axis in range(3):
        low, up = 2 * axis, 2 * axis + 1
        for k, other in ((low, up), (up, low)):
            match = (cols[other] == rows[k]).astype(jnp.int32)
            has = jnp.sum(match, axis=0, keepdims=True)
            place = jnp.sum(match * (other * count + sub), axis=0, keepdims=True)
            local = rows[k] - base
            if axis == 2:
                idx[k : k + 1, 0:count] = place
                idx[6 + k : 7 + k, 0:count] = local
                continue
            match_c = (cols[k] == rows[other]).astype(jnp.int32)
            has_c = jnp.sum(match_c, axis=1, keepdims=True)
            before = jnp.where((has_c == 0) & (cols[k] < rows[k]), 1, 0)
            rank = jnp.sum(before, axis=0, keepdims=True)
            before_c = jnp.where((has == 0) & (rows[k] < cols[k]), 1, 0)
            rank_c = jnp.sum(before_c, axis=1, keepdims=True)
            chosen = (has_c == 0) & (rank_c == lane)
            listed = jnp.sum(jnp.where(chosen, k * count + sub, 0), axis=0, keepdims=True)
            idx[k : k + 1, 0:count] = jnp.where(has > 0, place, starts[k] + rank)
            if k == low:
                traces = jnp.where(chosen, cols[k] - base, 0)
                idx[17 + axis : 18 + axis, 0:count] = jnp.sum(traces, axis=0, keepdims=True)
                idx[6 + k : 7 + k, 0:count] = local
            else:
                first = face_dev + (0 if axis == 0 else nx)
                idx[6 + k : 7 + k, 0:count] = jnp.where(has > 0, local, first + rank)
            idx[12 + k : 13 + k, 0:count] = listed
    wide = lax.broadcasted_iota(jnp.int32, (count, LANES), 1)
    wide_sub = lax.broadcasted_iota(jnp.int32, (count, LANES), 0)
    inverse = jnp.zeros((1, LANES), jnp.int32)
    for k in (0, 2, 4):
        owned = (cols[k] - base) == wide
        inverse = inverse + jnp.sum(
            jnp.where(owned, k * count + wide_sub, 0), axis=0, keepdims=True
        )
    idx[16:17, :] = inverse
    idx[0:6, :] = jnp.clip(idx[0:6, :], 0, slots + 2 * (nx + ny) - 1)
    idx[6:12, :] = jnp.clip(idx[6:12, :], 0, face_dev + nx + ny - 1)
    idx[12:17, :] = jnp.clip(idx[12:17, :], 0, slots - 1)
    idx[17:19, :] = jnp.clip(idx[17:19, :], 0, face_dev - 1)


def make_kernel(outer, inner, count, face_dev, groups, nx, ny):
    slots = 6 * count
    lows = (0, 2, 4)
    parts = outer * inner

    def kernel(heat_hbm, faces_hbm, stiff_ref, sol_ref, res_ref,
               heat_ref, faces_ref, raw, high, low, diag, tile_rows, table, v0, v1, v2, flux, flux2, q1,
               idx_v, idx, send0, recv0, sends, recvs, sum_tx, sum_rx,
               in_sem, raw_sem, idx_sem, s0_sem, r0_sem, ss_sem, rr_sem,
               sum_ss, sum_rs):
        gx = lax.axis_index("gx")
        gy = lax.axis_index("gy")
        x_next = (lax.rem(gx + 1, outer), gy)
        x_prev = (lax.rem(gx + outer - 1, outer), gy)
        y_next = (gx, lax.rem(gy + 1, inner))
        y_prev = (gx, lax.rem(gy + inner - 1, inner))

        get_heat = pltpu.make_async_copy(heat_hbm, heat_ref, in_sem.at[0])
        get_faces = pltpu.make_async_copy(faces_hbm, faces_ref, in_sem.at[1])
        get_faces.start()
        get_heat.start()

        def other(d):
            return (lax.rem(gx + d // inner, outer), lax.rem(gy + d % inner, inner))

        def raw_copy(e):
            return pltpu.make_async_copy(stiff_ref.at[e], raw.at[e], raw_sem.at[e])

        for e in range(count):
            raw_copy(e).start()
        barrier = pltpu.get_barrier_semaphore()
        for d in range(1, parts):
            pl.semaphore_signal(barrier, inc=1, device_id=other(d), device_id_type=MESH)

        base = (gx * inner + gy) * face_dev
        get_faces.wait()
        index_tables(faces_ref[...], base, count, face_dev, nx, ny, idx_v)
        to_smem = pltpu.make_async_copy(idx_v, idx, idx_sem)
        to_smem.start()
        get_heat.wait()
        for g in range(face_dev // 8):
            for j in range(groups):
                tile_rows[(g * groups + j) * 8 : (g * groups + j + 1) * 8, :] = heat_ref[
                    g * 8 : g * 8 + 8, j * LANES : (j + 1) * LANES
                ]
        for f in range(face_dev):
            start = (f // 8) * groups * 8 + f % 8
            table[f] = tile_rows[pl.ds(start, groups, stride=8), :]
        to_smem.wait()
        for r in range(nx):
            send0[r] = table[idx[17, r]]
        for r in range(ny):
            send0[nx + r] = table[idx[18, r]]
        pl.semaphore_wait(barrier, parts - 1)

        def remote(src, dst, ssem, rsem, device):
            return pltpu.make_async_remote_copy(
                src_ref=src, dst_ref=dst, send_sem=ssem, recv_sem=rsem,
                device_id=device, device_id_type=MESH,
            )

        first = [
            remote(send0.at[pl.ds(0, nx)], recv0.at[pl.ds(0, nx)], s0_sem.at[0], r0_sem.at[0], x_prev),
            remote(send0.at[pl.ds(nx, ny)], recv0.at[pl.ds(nx, ny)], s0_sem.at[1], r0_sem.at[1], y_prev),
        ]
        for c in first:
            c.start()

        eye = lax.broadcasted_iota(jnp.int32, (LANES, LANES), 0) == lax.broadcasted_iota(
            jnp.int32, (LANES, LANES), 1
        )

        def split(e, carry):
            raw_copy(e).wait()
            for r in range(3):
                rows = pl.ds(r * LANES, LANES)
                for c in range(3):
                    columns = pl.ds(c * LANES, LANES)
                    a = raw[e, rows, columns]
                    if r == c:
                        diag[e, :, columns] = jnp.sum(
                            jnp.where(eye, a, 0.0), axis=0, keepdims=True
                        )
                        a = jnp.where(eye, 0.0, a)
                    h = a.astype(BF16)
                    high[e, rows, columns] = h
                    low[e, rows, columns] = (a - h.astype(F32)).astype(BF16)
            return carry

        lax.fori_loop(0, count, split, 0)
        left = lax.broadcasted_iota(jnp.int32, (8, LANES), 1) < HALF

        def swap(a):
            return pltpu.roll(a, HALF, 1)

        def product(tiles, e):
            evens, odds = [], []
            for a, b in zip(tiles[0::2], tiles[1::2]):
                evens.append(jnp.where(left, a, swap(b)))
                odds.append(jnp.where(left, swap(a), b))
            x = jnp.concatenate(
                [jnp.concatenate(evens, axis=1), jnp.concatenate(odds, axis=1)], axis=0
            )
            depth = x.shape[1]
            xh = x.astype(BF16)
            xl = (x - xh.astype(F32)).astype(BF16)
            both = jnp.concatenate([xh, xl], axis=0)
            p = jnp.dot(both, high[e, 0:depth, :], preferred_element_type=F32)
            q = jnp.dot(xh, low[e, 0:depth, :], preferred_element_type=F32)
            y = p[0:16] + (p[16:32] + q)
            own = x * diag[e, :, 0:depth]
            out = []
            for axis in range(3):
                at = slice(axis * LANES, (axis + 1) * LANES)
                part = y[:, at] + own[:, at] if axis * LANES < depth else y[:, at]
                ev, od = part[0:8], part[8:16]
                out.append(jnp.where(left, ev, swap(od)))
                out.append(jnp.where(left, swap(ev), od))
            return out

        def inside(new, tiles_of, init):
            def body(e, acc):
                tiles, acc = tiles_of(e, acc)
                for k, f in enumerate(product(tiles, e)):
                    new[k * count + e] = f
                return acc

            return lax.fori_loop(0, count, body, init, unroll=True)

        def edges(new, tiles_of, init):
            def body(e, carry):
                dot, acc = carry
                tiles, full, acc = tiles_of(e, acc)
                for k, f in enumerate(product(tiles, e)):
                    s = k * count + e
                    f = new[s] + f
                    new[s] = f
                    dot = dot + f * full[k]
                return dot, acc

            start = (jnp.zeros((8, LANES), F32), init)
            return lax.fori_loop(0, count, body, start, unroll=True)

        spots = [0, nx, 2 * nx, 2 * nx + ny]
        plan = [(0, nx, x_prev, 1), (1, nx, x_next, 0), (2, ny, y_prev, 3), (3, ny, y_next, 2)]

        def exchange(phase, flux, kinds):
            copies = []
            for kind, rows, target, lands in plan:
                if kind not in kinds:
                    continue
                for r in range(rows):
                    sends[phase, spots[kind] + r] = flux[idx[12 + kind, r]]
                copies.append(
                    remote(
                        sends.at[phase, pl.ds(spots[kind], rows)],
                        recvs.at[phase, pl.ds(spots[lands], rows)],
                        ss_sem.at[phase, kind], rr_sem.at[phase, lands], target,
                    )
                )
                copies[-1].start()
            return copies

        def landed(phase, flux, copies, kinds):
            for c in copies:
                c.wait_recv()
            for kind, rows, _, _ in plan:
                if kind in kinds:
                    for r in range(rows):
                        flux[slots + spots[kind] + r] = recvs[phase, spots[kind] + r]

        def halves(tile):
            even = jnp.sum(jnp.where(left, tile, 0.0), axis=1, keepdims=True)
            odd = jnp.sum(jnp.where(left, 0.0, tile), axis=1, keepdims=True)
            return even, odd

        lane = lax.broadcasted_iota(jnp.int32, (8, LANES), 1)

        sub = lax.broadcasted_iota(jnp.int32, (8, LANES), 0)
        spot = lane % 16
        mine = lane // 16 == sub

        def packed(tiles, out=None, first=0):
            out = jnp.zeros((8, LANES), F32) if out is None else out
            for m, t in enumerate(tiles, first):
                even, odd = halves(t)
                out = jnp.where(spot == 2 * m, even, out)
                out = jnp.where(spot == 2 * m + 1, odd, out)
            return out

        def unpacked(row, m):
            own = jnp.where(mine, jnp.broadcast_to(row, (8, LANES)), 0.0)
            even = jnp.sum(jnp.where(spot == 2 * m, own, 0.0), axis=1, keepdims=True)
            odd = jnp.sum(jnp.where(spot == 2 * m + 1, own, 0.0), axis=1, keepdims=True)
            return jnp.where(left, even, odd)

        def sum_start(turn, value):
            sum_tx[turn] = jnp.sum(jnp.where(mine, value, 0.0), axis=0, keepdims=True)
            copies = []
            for d in range(1, parts):
                copies.append(remote(sum_tx.at[turn], sum_rx.at[turn, d - 1], sum_ss.at[turn, d - 1],
                                     sum_rs.at[turn, d - 1], other(d)))
                copies[-1].start()
            return copies

        def sum_end(turn, copies):
            for c in copies:
                c.wait_recv()
            return sum_tx[turn] + jnp.sum(sum_rx[turn], axis=0)

        zero = jnp.zeros((8, LANES), F32)

        every = (0, 1, 2, 3)

        def traces_in(e, acc):
            tiles = []
            for k in range(6):
                at = idx[6 + k, e]
                t = table[at]
                if k in (1, 3):
                    t = jnp.where(at < face_dev, t, 0.0)
                if k in lows:
                    acc = acc + t * t
                v0[k * count + e] = t
                tiles.append(t)
            return tiles, acc

        def traces_edge(e, acc):
            tiles, full = [], [v0[k * count + e] for k in range(6)]
            for k in range(4):
                t = zero
                if k in (1, 3):
                    at = idx[6 + k, e]
                    t = jnp.where(at < face_dev, 0.0, table[at])
                    full[k] = full[k] + t
                    v0[k * count + e] = full[k]
                tiles.append(t)
            return tiles, full, acc

        gamma0 = inside(flux, traces_in, zero)
        for c in first:
            c.wait_recv()
        for r in range(nx + ny):
            table[face_dev + r] = recv0[r]
        delta0, _ = edges(flux, traces_edge, 0)
        swap1 = exchange(0, flux, every)
        sum1 = sum_start(0, packed([gamma0, delta0]))

        def one_in(e, acc):
            tiles = []
            for k in range(6):
                s = k * count + e
                at = idx[k, e]
                t = flux[s] + flux[at]
                if k < 4:
                    t = jnp.where(at < slots, t, 0.0)
                v1[s] = t
                tiles.append(t)
            return tiles, acc

        def one_edge(e, acc):
            tiles, full = [], [v1[k * count + e] for k in range(6)]
            for k in range(4):
                s = k * count + e
                at = idx[k, e]
                t = jnp.where(at < slots, 0.0, flux[s] + flux[at])
                full[k] = full[k] + t
                v1[s] = full[k]
                tiles.append(t)
            return tiles, full, acc

        inside(flux2, one_in, 0)
        landed(0, flux, swap1, every)
        dot_g, _ = edges(flux2, one_edge, 0)
        swap2 = exchange(1, flux2, every)
        total = sum_end(0, sum1)
        gamma0 = unpacked(total, 0)
        delta0 = unpacked(total, 1)
        alpha0 = gamma0 / delta0

        def dots_of(s, val, w, acc):
            one = v1[s]
            r1 = v0[s] - alpha0 * one
            terms = (r1 * r1, r1 * w, w * w, w * one, one * one, w * val)
            return tuple(a + t for a, t in zip(acc, terms))

        def two_in(e, acc):
            tiles = []
            for k in range(6):
                s = k * count + e
                at = idx[k, e]
                val = flux2[s] + flux2[at]
                w = v1[s] - alpha0 * val
                if k < 4:
                    w = jnp.where(at < slots, w, 0.0)
                if k == 4:
                    acc = dots_of(s, val, w, acc)
                v2[s] = val
                q1[s] = w
                tiles.append(w)
            return tiles, acc

        def two_edge(e, acc):
            tiles, full = [], [q1[k * count + e] for k in range(6)]
            for k in range(4):
                s = k * count + e
                at = idx[k, e]
                val = flux2[s] + flux2[at]
                w = v1[s] - alpha0 * val
                tiles.append(jnp.where(at < slots, 0.0, w))
                full[k] = w
                if k in lows:
                    v2[s] = val
                    acc = dots_of(s, val, w, acc)
            return tiles, full, acc

        dots = inside(flux, two_in, (zero,) * 6)
        landed(1, flux2, swap2, every)
        dot_e, dots = edges(flux, two_edge, dots)
        early = packed([*dots, dot_g])
        sum2 = sum_start(1, packed([dot_e], early, 7))
        swap3 = exchange(2, flux, (1, 3))
        landed(2, flux, swap3, (0, 2))

        def asm3(e, carry):
            for k in lows:
                s = k * count + e
                flux[s] = flux[s] + flux[idx[k, e]]
            return carry

        lax.fori_loop(0, count, asm3, 0, unroll=UNROLL)
        total = sum_end(1, sum2)
        g1, d1, ww, wv, vv, f, g, ee = [unpacked(total, m) for m in range(8)]
        rv = -g1 / alpha0
        b0 = g1 / gamma0
        pap = d1 + 2.0 * b0 * rv + b0 * b0 * delta0
        a1 = g1 / pap
        rs = d1 + b0 * rv
        s2 = ww + b0 * (2.0 * wv + b0 * vv)
        g2 = g1 - 2.0 * a1 * rs + a1 * a1 * s2
        b1 = g2 / g1
        rar = d1 - 2.0 * a1 * (ww + b0 * wv) + a1 * a1 * (ee + b0 * (2.0 * f + b0 * g))
        pap2 = rar + 2.0 * b1 * (rs - a1 * s2) + b1 * b1 * pap
        a2 = g2 / pap2

        def finish(fc, carry):
            s = idx[16, fc]
            x0 = v0[s]
            one = v1[s]
            two = v2[s]
            r1 = x0 - alpha0 * one
            w = one - alpha0 * two
            p1 = r1 + b0 * x0
            s1 = w + b0 * one
            r2 = r1 - a1 * s1
            w2 = w - a1 * (flux[s] + b0 * two)
            p2 = r2 + b1 * p1
            sol_ref[fc] = alpha0 * x0 + a1 * p1 + a2 * p2
            res_ref[fc] = r2 - a2 * (w2 + b1 * s1)
            return carry

        lax.fori_loop(0, face_dev, finish, 0, unroll=2)
        for c in [*first, *swap1, *swap2, *swap3, *sum1, *sum2]:
            c.wait_send()

    return kernel


def local(heat_source, stiffness, element_faces):
    face_dev, width = heat_source.shape
    count, order = stiffness.shape[0], stiffness.shape[1]
    groups = width // LANES
    outer = lax.axis_size("gx")
    inner = lax.axis_size("gy")
    nx, ny = EY * EZ, EX * EZ
    slots = 6 * count
    ext = 2 * (nx + ny)
    tile = (groups, LANES)
    vmem = lambda *s: pltpu.VMEM(s, F32)
    dma = lambda *s: pltpu.SemaphoreType.DMA(s)
    out = jax.ShapeDtypeStruct((face_dev, *tile), F32)
    sol, res = pl.pallas_call(
        make_kernel(outer, inner, count, face_dev, groups, nx, ny),
        name="cg",
        out_shape=(out, out),
        in_specs=[
            pl.BlockSpec(memory_space=pltpu.HBM),
            pl.BlockSpec(memory_space=pltpu.HBM),
            pl.BlockSpec(memory_space=pltpu.HBM),
        ],
        out_specs=(pl.BlockSpec(memory_space=pltpu.VMEM),) * 2,
        scratch_shapes=[
            vmem(face_dev, width),
            pltpu.VMEM((6, count), jnp.int32),
            vmem(count, order, order),
            pltpu.VMEM((count, order, order), BF16),
            pltpu.VMEM((count, order, order), BF16),
            vmem(count, 1, order),
            vmem(face_dev * groups, LANES),
            vmem(face_dev + nx + ny, *tile),
            vmem(slots, *tile),
            vmem(slots, *tile),
            vmem(slots, *tile),
            vmem(slots + ext, *tile),
            vmem(slots + ext, *tile),
            vmem(slots, *tile),
            pltpu.VMEM((24, LANES), jnp.int32),
            pltpu.SMEM((24, LANES), jnp.int32),
            vmem(nx + ny, *tile),
            vmem(nx + ny, *tile),
            vmem(3, ext, *tile),
            vmem(3, ext, *tile),
            vmem(2, 1, LANES),
            vmem(2, outer * inner - 1, 1, LANES),
            dma(2),
            dma(count), pltpu.SemaphoreType.DMA,
            dma(2), dma(2), dma(3, 4), dma(3, 4),
            dma(2, outer * inner - 1), dma(2, outer * inner - 1),
        ],
        compiler_params=pltpu.CompilerParams(
            collective_id=0, has_side_effects=True, vmem_limit_bytes=67043328
        ),
    )(heat_source, element_faces.T, stiffness)
    return sol.reshape(face_dev, width), res.reshape(face_dev, width)


def solution(mesh):
    return jax.shard_map(
        local,
        mesh=mesh,
        in_specs=(P(("gx", "gy"), None), P(("gx", "gy"), None, None), P(("gx", "gy"), None)),
        out_specs=(P(("gx", "gy"), None), P(("gx", "gy"), None)),
        check_vma=False,
    )
```
